32 devices in a mesh: view: 4 (over y, core), row: 8 (over z, x).
Axes of the slice: x: 2, y: 2, z: 4, core: 2. Of those that a mesh axis runs over, the one named last changes fastest.
Arguments:
- features: float32 [4, 16384, 2048], P('view', 'row'), may hold values from -0.125 to 0.125
- view_maps: float32 [4, 2048, 256], P('view', 'row'), may hold values from -6 to 6
- shared: float32 [16384, 256], P('row'), may hold values from -6 to 6
Outputs:
- maps_out: float32 [4, 2048, 256], P('view', 'row')
- shared_out: float32 [16384, 256], P('row')
The draws below stay inside these ranges and needn't reach their ends.
All inputs are finite; a program needn't handle non-finite values.
Results may differ from the reference program's by a relative error of at most 0.00013.
Values sent between devices are 32-bit elements; how exact they have to be, the bound alone decides.
A program may use at most 128 MiB of HBM per device.

```python
import jax
import jax.numpy as jnp
from jax import lax

D = 2048
K = 256
ITERS = 2
NEWTON = 5
VIEWS = 4
TOTAL = 16384


def level_of(own_key, dims, split, smallest, top_value):
    def one(position, parts):
        heights = jax.random.uniform(jax.random.fold_in(jax.random.fold_in(own_key, 6), position), (parts,), jnp.float32, smallest / len(split), top_value / len(split))
        return jnp.repeat(jnp.exp(heights), dims[position] // parts).reshape((-1,) + (1,) * (len(dims) - position - 1))

    factor_of = one(*split[0])
    for cut in split[1:]:
        factor_of = factor_of * one(*cut)
    return factor_of


def centred(own_key, dims, scale, bound, split=(), kind=jnp.bfloat16):
    result = scale * jax.random.normal(own_key, dims, jnp.float32)
    if split:
        result = result * level_of(own_key, dims, split, -0.22, 0.18)
    return jnp.clip(result, -bound, bound).astype(kind)


def setup_inputs(seed: int = 0) -> dict:
    key_of = jax.random.split(jax.random.key(seed), 4)
    features = centred(key_of[0], (VIEWS, TOTAL, D), D ** -0.5, 0.125, ((0, 4), (1, 8)), jnp.float32)
    view_maps = centred(key_of[1], (VIEWS, D, K), 1.0, 6.0, ((0, 4), (1, 8)), jnp.float32)
    shared = centred(key_of[2], (TOTAL, K), 1.0, 6.0, ((0, 8),), jnp.float32)
    return {"features": features, "view_maps": view_maps, "shared": shared}


step_rate = 0.5

def newton_root(gram_matrix):
    highest = lax.Precision.HIGHEST
    frob_norm = jnp.sqrt(jnp.sum(gram_matrix * gram_matrix))
    scaled = gram_matrix / frob_norm
    identity = jnp.eye(gram_matrix.shape[0], dtype=jnp.float32)
    inverse_root = identity
    for newton_step in range(NEWTON):
        correction = 1.5 * identity - 0.5 * jnp.dot(inverse_root, scaled, precision=highest)
        scaled = jnp.dot(scaled, correction, precision=highest)
        inverse_root = jnp.dot(correction, inverse_root, precision=highest)
    return (inverse_root, frob_norm)

def reference(features, view_maps, shared):
    highest = lax.Precision.HIGHEST
    step_size = step_rate * D / TOTAL
    map_list = [view_maps[view_index] for view_index in range(VIEWS)]
    projected = [jnp.dot(features[view_index], map_list[view_index], precision=highest) for view_index in range(VIEWS)]
    for iteration in range(ITERS):
        for view_index in range(VIEWS):
            residual = projected[view_index] - shared
            gradient = jnp.dot(features[view_index].T, residual, precision=highest)
            map_list[view_index] = map_list[view_index] - step_size * gradient
            projected[view_index] = jnp.dot(features[view_index], map_list[view_index], precision=highest)
        summed = projected[0]
        for view_index in range(1, VIEWS):
            summed = summed + projected[view_index]
        average = summed / VIEWS
        gram_matrix = jnp.dot(average.T, average, precision=highest)
        inverse_root, frob_norm = newton_root(gram_matrix)
        shared = jnp.dot(average, inverse_root, precision=highest) * jnp.sqrt(TOTAL / frob_norm)
    return (jnp.stack(map_list, axis=0), shared)
```

```python
import functools
import math

import jax
import jax.numpy as jnp
from jax import lax
from jax.experimental import pallas as pl
from jax.experimental.pallas import tpu as pltpu
from jax.sharding import PartitionSpec as P

ITERS = 2
NEWTON = 5
STEP_RATE = 0.5
CORES = 2
MESH = pl.DeviceIdType.MESH
F32 = jnp.float32
BF16 = jnp.bfloat16


def split(x):
    hi = x.astype(BF16)
    return hi, (x - hi.astype(F32)).astype(BF16)


def dot3s(a, b):
    lhs = jnp.concatenate([a[0], a[1], a[0]], axis=1)
    rhs = jnp.concatenate([b[0], b[0], b[1]], axis=0)
    return jnp.dot(lhs, rhs, preferred_element_type=F32)


def dot3(a, b):
    return dot3s(split(a), split(b))


def newton_root(gram):
    size = gram.shape[0]
    frob = jnp.sqrt(jnp.sum(gram * gram, keepdims=True))
    scaled = gram / frob
    rows = lax.broadcasted_iota(jnp.int32, (size, size), 0)
    cols = lax.broadcasted_iota(jnp.int32, (size, size), 1)
    eye = jnp.where(rows == cols, 1.0, 0.0).astype(F32)
    root = None
    for step in range(NEWTON):
        ym = split(scaled)
        zy = scaled if root is None else dot3s(split(root), ym)
        corr = 1.5 * eye - 0.5 * zy
        cs = split(corr)
        if step < NEWTON - 1:
            scaled = dot3s(ym, cs)
        root = corr if root is None else dot3s(cs, split(root))
    return root, frob


def kernel(
    dims,
    f_ref, w_ref, s_ref, wo_ref, so_ref,
    fhi, flo, fbuf, rthi, rtlo, y, wfull, gs, xr, zs, zr,
    vs, cr, yr, av, gram, gr, gv, gfull,
    f_sem, agz_s, agz_r, agx_s, agx_r, rsx_s, rsx_r, rsz_s, rsz_r,
    vrc_s, vrc_r, vry_s, vry_r, vgy_s, vgy_r, vgc_s, vgc_r,
    g1_s, g1_r, g2_s, g2_r, g3_s, g3_r,
):
    nz, nx, ny, nc = dims
    nrow, nview = nz * nx, ny * nc
    row, view = lax.axis_index("row"), lax.axis_index("view")
    z, x = row // nx, row % nx
    yy, core = view // nc, view % nc
    local = y.shape[0]
    width = f_ref.shape[2]
    keys = y.shape[1]
    shard = w_ref.shape[1]
    total = local * nrow
    step_size = STEP_RATE * width / total
    chunk = fbuf.shape[1]
    nchunk = local // chunk
    part = local // nview
    gpart = keys // nrow

    def at_row(zz, xx):
        return {"row": zz * nx + xx}

    def at_view(y1, c1):
        return {"view": y1 * nc + c1}

    def zmod(d):
        return lax.rem(z + d + nz, nz)

    def xmod(d):
        return lax.rem(x + d + nx, nx)

    def ymod(d):
        return lax.rem(yy + d + ny, ny)

    def cmod(d):
        return lax.rem(core + d + nc, nc)

    pending = []

    def send(src, dst, ssem, rsem, dev):
        copy = pltpu.make_async_remote_copy(
            src_ref=src, dst_ref=dst, send_sem=ssem, recv_sem=rsem,
            device_id=dev, device_id_type=MESH,
        )
        copy.start()
        pending.append(copy)

    def recv(buf, ssem, rsem, dev):
        pltpu.make_async_remote_copy(
            src_ref=buf, dst_ref=buf, send_sem=ssem, recv_sem=rsem,
            device_id=dev, device_id_type=MESH,
        ).wait_recv()

    def flush():
        for copy in pending:
            copy.wait_send()
        pending.clear()

    def load(c):
        return pltpu.make_async_copy(
            f_ref.at[0, pl.ds(c * chunk, chunk)], fbuf.at[c % 2], f_sem.at[c % 2]
        )

    load(0).start()
    wfull[0, row] = w_ref[0]
    barrier = pltpu.get_barrier_semaphore()
    for d in range(1, nrow):
        pl.semaphore_signal(
            barrier, inc=1, device_id={"row": lax.rem(row + d, nrow)}, device_id_type=MESH
        )
    for d in range(1, nview):
        pl.semaphore_signal(
            barrier, inc=1, device_id={"view": lax.rem(view + d, nview)}, device_id_type=MESH
        )
    pl.semaphore_wait(barrier, nrow + nview - 2)

    def gather_start(g):
        own = wfull.at[g, row]
        for dx in range(1, nx):
            send(own, own, agx_s.at[g, 0, dx], agx_r.at[g, 0, dx], at_row(z, xmod(dx)))
        for dz in range(1, nz):
            send(own, own, agz_s.at[g, dz], agz_r.at[g, dz], at_row(zmod(dz), x))

    def project(g, block, first):
        ws = split(wfull[g, block])
        rhs = jnp.concatenate([ws[0], ws[0], ws[1]], axis=0)

        @pl.loop(0, local // 512)
        def _(c):
            rows = pl.ds(pl.multiple_of(c * 512, 512), 512)
            hi, lo = fhi[block, rows], flo[block, rows]
            out = jnp.dot(
                jnp.concatenate([hi, lo, hi], axis=1), rhs, preferred_element_type=F32
            )
            if first:
                y[rows] = out
            else:
                y[rows] += out

    def gather_project(g):
        project(g, row, True)
        for dz in range(nz):
            zsrc = zmod(-dz)
            if dz:
                block = zsrc * nx + x
                got = wfull.at[g, block]
                recv(got, agz_s.at[g, dz], agz_r.at[g, dz], at_row(zsrc, x))
                for dx in range(1, nx):
                    send(
                        got, got, agx_s.at[g, dz, dx], agx_r.at[g, dz, dx],
                        at_row(z, xmod(dx)),
                    )
                project(g, block, False)
            prev = dz - 1
            if prev >= 0:
                x_part(g, prev)
        x_part(g, nz - 1)

    def x_part(g, dz):
        for dx in range(1, nx):
            xsrc = xmod(-dx)
            block = zmod(-dz) * nx + xsrc
            recv(
                wfull.at[g, block], agx_s.at[g, dz, dx], agx_r.at[g, dz, dx],
                at_row(z, xsrc),
            )
            project(g, block, False)

    def set_residual(shared_of):
        @pl.loop(0, local // 512)
        def _(c):
            rows = pl.ds(pl.multiple_of(c * 512, 512), 512)
            res = (y[rows] - shared_of(c, rows)).T
            hi, lo = split(res)
            rthi[:, rows] = hi
            rtlo[:, rows] = lo

    def gradient(block):
        hi, lo = fhi[block], flo[block]
        rh = rthi[...]
        out = jnp.dot(rh, hi, preferred_element_type=F32)
        out += jnp.dot(rh, lo, preferred_element_type=F32)
        out += jnp.dot(rtlo[...], hi, preferred_element_type=F32)
        return out

    def scatter_gradient(it):
        order = list(range(1, nz)) + [0]
        for dz in order:
            for dx in range(1, nx):
                xt = xmod(dx)
                gs[it, dz, dx] = gradient(zmod(dz) * nx + xt)
                send(
                    gs.at[it, dz, dx], xr.at[it, dz, dx],
                    rsx_s.at[it, dz, dx], rsx_r.at[it, dz, dx], at_row(z, xt),
                )
        acc = None
        for dz in order:
            zs[it, dz] = gradient(zmod(dz) * nx + x)
            for dx in range(1, nx):
                recv(
                    xr.at[it, dz, dx], rsx_s.at[it, dz, dx], rsx_r.at[it, dz, dx],
                    at_row(z, xmod(-dx)),
                )
                zs[it, dz] += xr[it, dz, dx]
            if dz:
                send(
                    zs.at[it, dz], zr.at[it, dz], rsz_s.at[it, dz], rsz_r.at[it, dz],
                    at_row(zmod(dz), x),
                )
        acc = zs[it, 0]
        for dz in range(1, nz):
            recv(
                zr.at[it, dz], rsz_s.at[it, dz], rsz_r.at[it, dz], at_row(zmod(-dz), x)
            )
            acc = acc + zr[it, dz]
        wfull[it + 1, row] = wfull[it, row] - step_size * acc.T

    def yblock(block):
        return pl.ds(pl.multiple_of(block * part, part), part)

    def view_average(it):
        order = list(range(1, ny)) + [0]
        for dy in order:
            for dc in range(1, nc):
                ct = cmod(dc)
                send(
                    y.at[yblock(ymod(dy) * nc + ct)], cr.at[it, dy, dc],
                    vrc_s.at[it, dy, dc], vrc_r.at[it, dy, dc], at_view(yy, ct),
                )
        for dy in order:
            acc = y[yblock(ymod(dy) * nc + core)]
            for dc in range(1, nc):
                recv(
                    cr.at[it, dy, dc], vrc_s.at[it, dy, dc], vrc_r.at[it, dy, dc],
                    at_view(yy, cmod(-dc)),
                )
                acc = acc + cr[it, dy, dc]
            vs[it, dy] = acc
            if dy:
                send(
                    vs.at[it, dy], yr.at[it, dy], vry_s.at[it, dy], vry_r.at[it, dy],
                    at_view(ymod(dy), core),
                )
        acc = vs[it, 0]
        for dy in range(1, ny):
            recv(
                yr.at[it, dy], vry_s.at[it, dy], vry_r.at[it, dy],
                at_view(ymod(-dy), core),
            )
            acc = acc + yr[it, dy]
        acc = acc / nview
        av[it, view] = acc
        own = av.at[it, view]
        for dy in range(1, ny):
            send(
                own, own, vgy_s.at[it, dy], vgy_r.at[it, dy], at_view(ymod(dy), core)
            )
        for dc in range(1, nc):
            send(
                own, own, vgc_s.at[it, 0, dc], vgc_r.at[it, 0, dc], at_view(yy, cmod(dc))
            )

    def reduce_gram(it):
        own = av[it, view]
        hi, lo = split(own)
        thi, tlo = split(own.T)
        gram[it] = dot3s((thi, tlo), (hi, lo)).reshape(nrow, gpart, keys)
        for d in range(1, nrow):
            to = lax.rem(row + d, nrow)
            send(
                gram.at[it, to], gr.at[it, d], g1_s.at[it, d], g1_r.at[it, d], {"row": to}
            )
        acc = gram[it, row]
        for d in range(1, nrow):
            recv(
                gr.at[it, d], g1_s.at[it, d], g1_r.at[it, d],
                {"row": lax.rem(row - d + nrow, nrow)},
            )
            acc = acc + gr[it, d]
        gv[it, 0] = acc
        for d in range(1, nview):
            send(
                gv.at[it, 0], gv.at[it, d], g2_s.at[it, d], g2_r.at[it, d],
                {"view": lax.rem(view + d, nview)},
            )
        acc = gv[it, 0]
        for d in range(1, nview):
            recv(
                gv.at[it, d], g2_s.at[it, d], g2_r.at[it, d],
                {"view": lax.rem(view - d + nview, nview)},
            )
            acc = acc + gv[it, d]
        gfull[it, row] = acc
        mine = gfull.at[it, row]
        for d in range(1, nrow):
            send(
                mine, mine, g3_s.at[it, d], g3_r.at[it, d],
                {"row": lax.rem(row + d, nrow)},
            )

    def forward_average(it):
        for dy in range(1, ny):
            ysrc = ymod(-dy)
            got = av.at[it, ysrc * nc + core]
            recv(got, vgy_s.at[it, dy], vgy_r.at[it, dy], at_view(ysrc, core))
            for dc in range(1, nc):
                send(
                    got, got, vgc_s.at[it, dy, dc], vgc_r.at[it, dy, dc],
                    at_view(yy, cmod(dc)),
                )

    def finish_average(it):
        for dy in range(ny):
            for dc in range(1, nc):
                csrc = cmod(-dc)
                recv(
                    av.at[it, ymod(-dy) * nc + csrc],
                    vgc_s.at[it, dy, dc], vgc_r.at[it, dy, dc], at_view(yy, csrc),
                )

    def finish_gram(it):
        for d in range(1, nrow):
            src = lax.rem(row - d + nrow, nrow)
            recv(gfull.at[it, src], g3_s.at[it, d], g3_r.at[it, d], {"row": src})
        return newton_root(gfull[it].reshape(keys, keys))

    gather_start(0)
    for c in range(nchunk):
        if c + 1 < nchunk:
            load(c + 1).start()
        load(c).wait()
        for b in range(nrow):
            hi, lo = split(fbuf[c % 2, :, b * shard:(b + 1) * shard])
            fhi[b, c * chunk:(c + 1) * chunk] = hi
            flo[b, c * chunk:(c + 1) * chunk] = lo
    gather_project(0)
    set_residual(lambda c, rows: s_ref[rows])
    for it in range(ITERS):
        scatter_gradient(it)
        gather_start(it + 1)
        gather_project(it + 1)
        view_average(it)
        reduce_gram(it)
        forward_average(it)
        root, frob = finish_gram(it)
        scale = jnp.sqrt(total / frob)
        finish_average(it)
        flush()
        rs = split(root)
        if it < ITERS - 1:
            for v in range(nview):
                rows = slice(v * part, (v + 1) * part)
                hi, lo = split((y[rows] - dot3s(split(av[it, v]), rs) * scale).T)
                rthi[:, rows] = hi
                rtlo[:, rows] = lo
        else:
            for v in range(nview):
                so_ref[v * part:(v + 1) * part] = dot3s(split(av[it, v]), rs) * scale
            wo_ref[0] = wfull[ITERS, row]


def solution(mesh):
    nrow, nview = mesh.shape["row"], mesh.shape["view"]
    nx = max(d for d in range(1, math.isqrt(nrow) + 1) if nrow % d == 0)
    nz = nrow // nx
    nc = CORES if nview % CORES == 0 else 1
    ny = nview // nc

    def local(features, view_maps, shared):
        rows, width = features.shape[1], features.shape[2]
        shard, keys = view_maps.shape[1], view_maps.shape[2]
        part, gpart = rows // nview, keys // nrow
        chunk = 256
        dma = pltpu.SemaphoreType.DMA
        sems = []
        for shape in [
            (ITERS + 1, nz), (ITERS + 1, nz, nx), (ITERS, nz, nx), (ITERS, nz),
            (ITERS, ny, nc), (ITERS, ny), (ITERS, ny), (ITERS, ny, nc),
            (ITERS, nrow), (ITERS, nview), (ITERS, nrow),
        ]:
            sems += [dma(shape), dma(shape)]
        vmem = pl.BlockSpec(memory_space=pltpu.VMEM)
        return pl.pallas_call(
            functools.partial(kernel, (nz, nx, ny, nc)),
            out_shape=(
                jax.ShapeDtypeStruct(view_maps.shape, F32),
                jax.ShapeDtypeStruct(shared.shape, F32),
            ),
            in_specs=[pl.BlockSpec(memory_space=pl.ANY), vmem, vmem],
            out_specs=(vmem, vmem),
            scratch_shapes=[
                pltpu.VMEM((nrow, rows, shard), BF16),
                pltpu.VMEM((nrow, rows, shard), BF16),
                pltpu.VMEM((2, chunk, width), F32),
                pltpu.VMEM((keys, rows), BF16),
                pltpu.VMEM((keys, rows), BF16),
                pltpu.VMEM((rows, keys), F32),
                pltpu.VMEM((ITERS + 1, nrow, shard, keys), F32),
                pltpu.VMEM((ITERS, nz, nx, keys, shard), F32),
                pltpu.VMEM((ITERS, nz, nx, keys, shard), F32),
                pltpu.VMEM((ITERS, nz, keys, shard), F32),
                pltpu.VMEM((ITERS, nz, keys, shard), F32),
                pltpu.VMEM((ITERS, ny, part, keys), F32),
                pltpu.VMEM((ITERS, ny, nc, part, keys), F32),
                pltpu.VMEM((ITERS, ny, part, keys), F32),
                pltpu.VMEM((ITERS, nview, part, keys), F32),
                pltpu.VMEM((ITERS, nrow, gpart, keys), F32),
                pltpu.VMEM((ITERS, nrow, gpart, keys), F32),
                pltpu.VMEM((ITERS, nview, gpart, keys), F32),
                pltpu.VMEM((ITERS, nrow, gpart, keys), F32),
                dma((2,)),
            ] + sems,
            compiler_params=pltpu.CompilerParams(
                collective_id=0, has_side_effects=True, vmem_limit_bytes=67043328
            ),
        )(features, view_maps, shared)

    in_specs = (P("view", "row", None), P("view", "row", None), P("row", None))
    out_specs = (P("view", "row", None), P("row", None))
    return jax.shard_map(local, mesh=mesh, in_specs=in_specs, out_specs=out_specs, check_vma=False)
```

```python
import functools
import math

import jax
import jax.numpy as jnp
from jax import lax
from jax.experimental import pallas as pl
from jax.experimental.pallas import tpu as pltpu
from jax.sharding import PartitionSpec as P

ITERS = 2
NEWTON = 5
STEP_RATE = 0.5
CORES = 2
HALVES = 2
MESH = pl.DeviceIdType.MESH
F32 = jnp.float32
BF16 = jnp.bfloat16


def split(x):
    hi = x.astype(BF16)
    return hi, (x - hi.astype(F32)).astype(BF16)


def dot3s(a, b):
    lhs = jnp.concatenate([a[0], a[1], a[0]], axis=1)
    rhs = jnp.concatenate([b[0], b[0], b[1]], axis=0)
    return jnp.dot(lhs, rhs, preferred_element_type=F32)


def dot3(a, b):
    return dot3s(split(a), split(b))


def newton_root(gram):
    size = gram.shape[0]
    frob = jnp.sqrt(jnp.sum(gram * gram, keepdims=True))
    scaled = gram / frob
    rows = lax.broadcasted_iota(jnp.int32, (size, size), 0)
    cols = lax.broadcasted_iota(jnp.int32, (size, size), 1)
    eye = jnp.where(rows == cols, 1.0, 0.0).astype(F32)
    root = None
    for step in range(NEWTON):
        ym = split(scaled)
        zy = scaled if root is None else dot3s(split(root), ym)
        corr = 1.5 * eye - 0.5 * zy
        cs = split(corr)
        if step < NEWTON - 1:
            scaled = dot3s(ym, cs)
        root = corr if root is None else dot3s(cs, split(root))
    return root, frob


def kernel(
    dims,
    f_ref, w_ref, s_ref, wo_ref, so_ref,
    fhi, flo, fbuf, rthi, rtlo, y, wfull, gs, xr, zs, zr,
    vs, cr, yr, av, gram, gr, gv, gfull,
    f_sem, agz_s, agz_r, agx_s, agx_r, rsx_s, rsx_r, rsz_s, rsz_r,
    vrc_s, vrc_r, vry_s, vry_r, vgy_s, vgy_r, vgc_s, vgc_r,
    g1_s, g1_r, g2_s, g2_r, g3_s, g3_r,
):
    nz, nx, ny, nc = dims
    nrow, nview = nz * nx, ny * nc
    row, view = lax.axis_index("row"), lax.axis_index("view")
    z, x = row // nx, row % nx
    yy, core = view // nc, view % nc
    local = y.shape[1]
    width = f_ref.shape[2]
    half = y.shape[2]
    keys = HALVES * half
    shard = w_ref.shape[1]
    total = local * nrow
    step_size = STEP_RATE * width / total
    chunk = fbuf.shape[1]
    nchunk = local // chunk
    part = local // nview
    gpart = keys // nrow

    def at_row(zz, xx):
        return {"row": zz * nx + xx}

    def at_view(y1, c1):
        return {"view": y1 * nc + c1}

    def zmod(d):
        return lax.rem(z + d + nz, nz)

    def xmod(d):
        return lax.rem(x + d + nx, nx)

    def ymod(d):
        return lax.rem(yy + d + ny, ny)

    def cmod(d):
        return lax.rem(core + d + nc, nc)

    pending = []

    def send(src, dst, ssem, rsem, dev):
        copy = pltpu.make_async_remote_copy(
            src_ref=src, dst_ref=dst, send_sem=ssem, recv_sem=rsem,
            device_id=dev, device_id_type=MESH,
        )
        copy.start()
        pending.append(copy)

    def recv(buf, ssem, rsem, dev):
        pltpu.make_async_remote_copy(
            src_ref=buf, dst_ref=buf, send_sem=ssem, recv_sem=rsem,
            device_id=dev, device_id_type=MESH,
        ).wait_recv()

    def flush():
        for copy in pending:
            copy.wait_send()
        pending.clear()

    def load(c):
        return pltpu.make_async_copy(
            f_ref.at[0, pl.ds(c * chunk, chunk)], fbuf.at[c % 2], f_sem.at[c % 2]
        )

    load(0).start()
    for h in range(HALVES):
        wfull[0, h, row] = w_ref[0, :, h * half:(h + 1) * half]
    barrier = pltpu.get_barrier_semaphore()
    for d in range(1, nrow):
        pl.semaphore_signal(
            barrier, inc=1, device_id={"row": lax.rem(row + d, nrow)}, device_id_type=MESH
        )
    for d in range(1, nview):
        pl.semaphore_signal(
            barrier, inc=1, device_id={"view": lax.rem(view + d, nview)}, device_id_type=MESH
        )
    pl.semaphore_wait(barrier, nrow + nview - 2)

    def gather_start(g, h):
        own = wfull.at[g, h, row]
        for dx in range(1, nx):
            send(
                own, own, agx_s.at[g, h, 0, dx], agx_r.at[g, h, 0, dx],
                at_row(z, xmod(dx)),
            )
        for dz in range(1, nz):
            send(own, own, agz_s.at[g, h, dz], agz_r.at[g, h, dz], at_row(zmod(dz), x))

    def forward(g, h, dz):
        zsrc = zmod(-dz)
        got = wfull.at[g, h, zsrc * nx + x]
        recv(got, agz_s.at[g, h, dz], agz_r.at[g, h, dz], at_row(zsrc, x))
        for dx in range(1, nx):
            send(
                got, got, agx_s.at[g, h, dz, dx], agx_r.at[g, h, dz, dx],
                at_row(z, xmod(dx)),
            )

    def project(g, hs, block, first):
        parts = [split(wfull[g, h, block]) for h in hs]
        hi, lo = (jnp.concatenate(p, axis=1) for p in zip(*parts))
        rhs = jnp.concatenate([hi, hi, lo], axis=0)

        @pl.loop(0, local // 512)
        def _(c):
            rows = pl.ds(pl.multiple_of(c * 512, 512), 512)
            fh, fl = fhi[block, rows], flo[block, rows]
            out = jnp.dot(
                jnp.concatenate([fh, fl, fh], axis=1), rhs, preferred_element_type=F32
            )
            for i, h in enumerate(hs):
                piece = out[:, i * half:(i + 1) * half]
                if first:
                    y[h, rows] = piece
                else:
                    y[h, rows] += piece

    def x_part(g, hs, dz):
        for dx in range(1, nx):
            xsrc = xmod(-dx)
            block = zmod(-dz) * nx + xsrc
            for h in hs:
                recv(
                    wfull.at[g, h, block], agx_s.at[g, h, dz, dx], agx_r.at[g, h, dz, dx],
                    at_row(z, xsrc),
                )
            project(g, hs, block, False)

    def gather_project(g, hs, done=(), hook=None):
        project(g, hs, row, True)
        for dz in range(nz):
            if dz:
                for h in hs:
                    if (dz, h) not in done:
                        forward(g, h, dz)
                project(g, hs, zmod(-dz) * nx + x, False)
                x_part(g, hs, dz - 1)
                if hook is not None and dz == 1:
                    hook()
        x_part(g, hs, nz - 1)

    def set_residual(shared_of):
        @pl.loop(0, local // 512)
        def _(c):
            rows = pl.ds(pl.multiple_of(c * 512, 512), 512)
            mine = jnp.concatenate([y[h, rows] for h in range(HALVES)], axis=1)
            res = (mine - shared_of(c, rows)).T
            hi, lo = split(res)
            rthi[:, rows] = hi
            rtlo[:, rows] = lo

    def gradient(block):
        hi, lo = fhi[block], flo[block]
        rh = rthi[...]
        out = jnp.dot(rh, hi, preferred_element_type=F32)
        out += jnp.dot(rh, lo, preferred_element_type=F32)
        out += jnp.dot(rtlo[...], hi, preferred_element_type=F32)
        return out

    def scatter_gradient(it):
        order = list(range(1, nz)) + [0]
        for dz in order:
            for dx in range(1, nx):
                xt = xmod(dx)
                grad = gradient(zmod(dz) * nx + xt)
                for h in range(HALVES):
                    gs[it, h, dz, dx] = grad[h * half:(h + 1) * half]
                    send(
                        gs.at[it, h, dz, dx], xr.at[it, h, dz, dx],
                        rsx_s.at[it, h, dz, dx], rsx_r.at[it, h, dz, dx], at_row(z, xt),
                    )
        for dz in order:
            grad = gradient(zmod(dz) * nx + x)
            for h in range(HALVES):
                acc = grad[h * half:(h + 1) * half]
                for dx in range(1, nx):
                    recv(
                        xr.at[it, h, dz, dx], rsx_s.at[it, h, dz, dx],
                        rsx_r.at[it, h, dz, dx], at_row(z, xmod(-dx)),
                    )
                    acc = acc + xr[it, h, dz, dx]
                zs[it, h, dz] = acc
                if dz:
                    send(
                        zs.at[it, h, dz], zr.at[it, h, dz],
                        rsz_s.at[it, h, dz], rsz_r.at[it, h, dz], at_row(zmod(dz), x),
                    )
        for h in range(HALVES):
            acc = zs[it, h, 0]
            for dz in range(1, nz):
                recv(
                    zr.at[it, h, dz], rsz_s.at[it, h, dz], rsz_r.at[it, h, dz],
                    at_row(zmod(-dz), x),
                )
                acc = acc + zr[it, h, dz]
            wfull[it + 1, h, row] = wfull[it, h, row] - step_size * acc.T
            gather_start(it + 1, h)

    def yblock(block):
        return pl.ds(pl.multiple_of(block * part, part), part)

    yorder = list(range(1, ny)) + [0]

    def view_send(it, h):
        for dy in yorder:
            for dc in range(1, nc):
                ct = cmod(dc)
                send(
                    y.at[h, yblock(ymod(dy) * nc + ct)], cr.at[it, h, dy, dc],
                    vrc_s.at[it, h, dy, dc], vrc_r.at[it, h, dy, dc], at_view(yy, ct),
                )

    def view_mid(it, h):
        for dy in yorder:
            acc = y[h, yblock(ymod(dy) * nc + core)]
            for dc in range(1, nc):
                recv(
                    cr.at[it, h, dy, dc], vrc_s.at[it, h, dy, dc], vrc_r.at[it, h, dy, dc],
                    at_view(yy, cmod(-dc)),
                )
                acc = acc + cr[it, h, dy, dc]
            vs[it, h, dy] = acc
            if dy:
                send(
                    vs.at[it, h, dy], yr.at[it, h, dy],
                    vry_s.at[it, h, dy], vry_r.at[it, h, dy], at_view(ymod(dy), core),
                )

    def view_end(it, h):
        acc = vs[it, h, 0]
        for dy in range(1, ny):
            recv(
                yr.at[it, h, dy], vry_s.at[it, h, dy], vry_r.at[it, h, dy],
                at_view(ymod(-dy), core),
            )
            acc = acc + yr[it, h, dy]
        av[it, h, view] = acc / nview
        own = av.at[it, h, view]
        for dy in range(1, ny):
            send(
                own, own, vgy_s.at[it, h, dy], vgy_r.at[it, h, dy],
                at_view(ymod(dy), core),
            )
        for dc in range(1, nc):
            send(
                own, own, vgc_s.at[it, h, 0, dc], vgc_r.at[it, h, 0, dc],
                at_view(yy, cmod(dc)),
            )

    def ypart(rows):
        return jnp.concatenate([y[h, rows] for h in range(HALVES)], axis=1)

    def average(it, v):
        return jnp.concatenate([av[it, h, v] for h in range(HALVES)], axis=1)

    def reduce_gram(it):
        own = average(it, view)
        hi, lo = split(own)
        thi, tlo = split(own.T)
        gram[it] = dot3s((thi, tlo), (hi, lo)).reshape(nrow, gpart, keys)
        for d in range(1, nrow):
            to = lax.rem(row + d, nrow)
            send(
                gram.at[it, to], gr.at[it, d], g1_s.at[it, d], g1_r.at[it, d], {"row": to}
            )
        acc = gram[it, row]
        for d in range(1, nrow):
            recv(
                gr.at[it, d], g1_s.at[it, d], g1_r.at[it, d],
                {"row": lax.rem(row - d + nrow, nrow)},
            )
            acc = acc + gr[it, d]
        gv[it, 0] = acc
        for d in range(1, nview):
            send(
                gv.at[it, 0], gv.at[it, d], g2_s.at[it, d], g2_r.at[it, d],
                {"view": lax.rem(view + d, nview)},
            )
        acc = gv[it, 0]
        for d in range(1, nview):
            recv(
                gv.at[it, d], g2_s.at[it, d], g2_r.at[it, d],
                {"view": lax.rem(view - d + nview, nview)},
            )
            acc = acc + gv[it, d]
        gfull[it, row] = acc
        mine = gfull.at[it, row]
        for d in range(1, nrow):
            send(
                mine, mine, g3_s.at[it, d], g3_r.at[it, d],
                {"row": lax.rem(row + d, nrow)},
            )

    def forward_average(it):
        for h in range(HALVES):
            for dy in range(1, ny):
                ysrc = ymod(-dy)
                got = av.at[it, h, ysrc * nc + core]
                recv(got, vgy_s.at[it, h, dy], vgy_r.at[it, h, dy], at_view(ysrc, core))
                for dc in range(1, nc):
                    send(
                        got, got, vgc_s.at[it, h, dy, dc], vgc_r.at[it, h, dy, dc],
                        at_view(yy, cmod(dc)),
                    )

    def finish_average(it):
        for h in range(HALVES):
            for dy in range(ny):
                for dc in range(1, nc):
                    csrc = cmod(-dc)
                    recv(
                        av.at[it, h, ymod(-dy) * nc + csrc],
                        vgc_s.at[it, h, dy, dc], vgc_r.at[it, h, dy, dc],
                        at_view(yy, csrc),
                    )

    def finish_gram(it):
        for d in range(1, nrow):
            src = lax.rem(row - d + nrow, nrow)
            recv(gfull.at[it, src], g3_s.at[it, d], g3_r.at[it, d], {"row": src})
        return newton_root(gfull[it].reshape(keys, keys))

    for h in range(HALVES):
        gather_start(0, h)
    early = [(dz, h) for dz in range(1, nz - 1) for h in range(HALVES)]
    done = []
    for c in range(nchunk):
        if c + 1 < nchunk:
            load(c + 1).start()
        load(c).wait()
        for b in range(nrow):
            hi, lo = split(fbuf[c % 2, :, b * shard:(b + 1) * shard])
            fhi[b, c * chunk:(c + 1) * chunk] = hi
            flo[b, c * chunk:(c + 1) * chunk] = lo
        if c >= 2 and len(done) < len(early):
            dz, h = early[len(done)]
            forward(0, h, dz)
            done.append((dz, h))
    gather_project(0, tuple(range(HALVES)), done)
    set_residual(lambda c, rows: s_ref[rows])
    for it in range(ITERS):
        scatter_gradient(it)
        hook = None
        for h in range(HALVES):
            gather_project(it + 1, (h,), hook=hook)
            view_send(it, h)
            hook = functools.partial(view_mid, it, h)
        hook()
        for h in range(HALVES):
            view_end(it, h)
        reduce_gram(it)
        forward_average(it)
        root, frob = finish_gram(it)
        scale = jnp.sqrt(total / frob)
        finish_average(it)
        flush()
        rs = split(root)
        if it < ITERS - 1:
            for v in range(nview):
                rows = slice(v * part, (v + 1) * part)
                hi, lo = split((ypart(rows) - dot3s(split(average(it, v)), rs) * scale).T)
                rthi[:, rows] = hi
                rtlo[:, rows] = lo
        else:
            for v in range(nview):
                so_ref[v * part:(v + 1) * part] = dot3s(split(average(it, v)), rs) * scale
            for h in range(HALVES):
                wo_ref[0, :, h * half:(h + 1) * half] = wfull[ITERS, h, row]


def solution(mesh):
    nrow, nview = mesh.shape["row"], mesh.shape["view"]
    nx = max(d for d in range(1, math.isqrt(nrow) + 1) if nrow % d == 0)
    nz = nrow // nx
    nc = CORES if nview % CORES == 0 else 1
    ny = nview // nc

    def local(features, view_maps, shared):
        rows, width = features.shape[1], features.shape[2]
        shard, keys = view_maps.shape[1], view_maps.shape[2]
        part, gpart, half = rows // nview, keys // nrow, keys // HALVES
        chunk = 256
        dma = pltpu.SemaphoreType.DMA
        sems = []
        for shape in [
            (ITERS + 1, HALVES, nz), (ITERS + 1, HALVES, nz, nx),
            (ITERS, HALVES, nz, nx), (ITERS, HALVES, nz),
            (ITERS, HALVES, ny, nc), (ITERS, HALVES, ny),
            (ITERS, HALVES, ny), (ITERS, HALVES, ny, nc),
            (ITERS, nrow), (ITERS, nview), (ITERS, nrow),
        ]:
            sems += [dma(shape), dma(shape)]
        vmem = pl.BlockSpec(memory_space=pltpu.VMEM)
        return pl.pallas_call(
            functools.partial(kernel, (nz, nx, ny, nc)),
            out_shape=(
                jax.ShapeDtypeStruct(view_maps.shape, F32),
                jax.ShapeDtypeStruct(shared.shape, F32),
            ),
            in_specs=[pl.BlockSpec(memory_space=pl.ANY), vmem, vmem],
            out_specs=(vmem, vmem),
            scratch_shapes=[
                pltpu.VMEM((nrow, rows, shard), BF16),
                pltpu.VMEM((nrow, rows, shard), BF16),
                pltpu.VMEM((2, chunk, width), F32),
                pltpu.VMEM((keys, rows), BF16),
                pltpu.VMEM((keys, rows), BF16),
                pltpu.VMEM((HALVES, rows, half), F32),
                pltpu.VMEM((ITERS + 1, HALVES, nrow, shard, half), F32),
                pltpu.VMEM((ITERS, HALVES, nz, nx, half, shard), F32),
                pltpu.VMEM((ITERS, HALVES, nz, nx, half, shard), F32),
                pltpu.VMEM((ITERS, HALVES, nz, half, shard), F32),
                pltpu.VMEM((ITERS, HALVES, nz, half, shard), F32),
                pltpu.VMEM((ITERS, HALVES, ny, part, half), F32),
                pltpu.VMEM((ITERS, HALVES, ny, nc, part, half), F32),
                pltpu.VMEM((ITERS, HALVES, ny, part, half), F32),
                pltpu.VMEM((ITERS, HALVES, nview, part, half), F32),
                pltpu.VMEM((ITERS, nrow, gpart, keys), F32),
                pltpu.VMEM((ITERS, nrow, gpart, keys), F32),
                pltpu.VMEM((ITERS, nview, gpart, keys), F32),
                pltpu.VMEM((ITERS, nrow, gpart, keys), F32),
                dma((2,)),
            ] + sems,
            compiler_params=pltpu.CompilerParams(
                collective_id=0, has_side_effects=True, vmem_limit_bytes=67043328
            ),
        )(features, view_maps, shared)

    in_specs = (P("view", "row", None), P("view", "row", None), P("row", None))
    out_specs = (P("view", "row", None), P("row", None))
    return jax.shard_map(local, mesh=mesh, in_specs=in_specs, out_specs=out_specs, check_vma=False)
```
